128 devices in a mesh: row: 8 (over x_lo, y), col: 16 (over x_hi, z, core).
Axes of the slice: x: 4 (x_hi: 2, x_lo: 2; x = x_hi * 2 + x_lo), y: 4, z: 4, core: 2. Of those that a mesh axis runs over, the one named last changes fastest.
Arguments:
- features: bfloat16 [262144, 256], P(('col', 'row')), may hold values from -6 to 6
- weight: bfloat16 [256, 256], replicated, may hold values from -0.375 to 0.375
- adj_rows: int32 [8, 16, 128], P('row', 'col'), may hold values from 0 to 255, as said below
- adj_cols: int32 [8, 16, 128], P('row', 'col'), may hold values from 0 to 127
- adj_blocks: bfloat16 [8, 16, 128, 128, 128], P('row', 'col'), as said below
- counts: int32 [8, 16], P('row', 'col'), may hold values from 1 to 128, as said below
- grad_out: bfloat16 [262144, 256], P(('col', 'row')), may hold values from -6 to 6
Outputs:
- out_col: bfloat16 [262144, 256], P(('col', 'row'))
- weight_grad: float32 [256, 256], replicated
The draws below stay inside these ranges and needn't reach their ends.
Inputs may be any that keep to these rules, and one draw needn't show every extreme that they name: `adj_rows`: in every grid cell, slot k's block-row lies in [(k % 16) * 16, (k % 16 + 1) * 16), and no two slots of a cell share a block-row. At least one grid cell has all 128 slots live; live slots are the first counts of a cell. `adj_blocks`: each block holds nonnegative edge weights.
All inputs are finite; a program needn't handle non-finite values.
Results may differ from the reference program's by a relative error of at most 0.015.
Values may be sent and summed in bfloat16 or wider, within the bound.
No kernel may reach another device: no remote copies, remote signals or barrier semaphores. Data moves between devices by JAX's collectives and lax.ppermute only.
A program may use at most 128 MiB of HBM per device.

```python
import jax
import jax.numpy as jnp
from jax import lax

F = 256
BS = 128
VBLK = 16
SLOTS = 128
RB = 256
CB = 128
NVERT = 262144
SUB = 16
N_ROW = 8
N_COL = 16
DEVICES = 128


def slot_rows(key):
    per_owner = SLOTS // N_COL
    scores = jax.random.randint(jax.random.fold_in(key, 21), (N_ROW, N_COL, N_COL, VBLK), 0, 1048576)
    ranked = scores * VBLK + jnp.arange(VBLK, dtype=jnp.int32)
    order = jnp.argsort(ranked, axis=-1)[..., :per_owner].astype(jnp.int32)
    owners = jnp.arange(N_COL, dtype=jnp.int32)[None, None, :, None]
    picked = owners * VBLK + order
    return picked.transpose(0, 1, 3, 2).reshape(N_ROW, N_COL, SLOTS).astype(jnp.int32)


def draw_adj_rows(key, part):
    return slot_rows(key)


def draw_adj_cols(key, part):
    rows = slot_rows(key)
    home = rows * CB // RB
    offset = jax.random.randint(jax.random.fold_in(key, 31), rows.shape, -2, 3)
    return jnp.clip(home + offset, 0, CB - 1).astype(jnp.int32)


def draw_adj_blocks(key, part):
    share = min(0.5, 16.0 / BS)
    shape = (N_ROW, N_COL, SLOTS, BS, BS)
    keep = jax.random.uniform(jax.random.fold_in(key, 41), shape, jnp.float32) < share
    values = jax.random.uniform(jax.random.fold_in(key, 42), shape, jnp.float32, 0.5, 1.5) * (2.0 * share * BS) ** (-0.5)
    return jnp.where(keep, values, 0.0).astype(jnp.bfloat16)


def draw_counts(key, part):
    row_ids = jnp.arange(N_ROW, dtype=jnp.int32)[:, None]
    col_ids = jnp.arange(N_COL, dtype=jnp.int32)[None, :]
    distance = jnp.abs((2 * col_ids + 1) * N_ROW - (2 * row_ids + 1) * N_COL) // (2 * N_ROW)
    halving = jnp.minimum(distance, 3)
    divisor = jnp.array([1, 2, 4, 8], jnp.int32)[halving]
    ceiling = SLOTS // divisor
    jitter = jax.random.randint(jax.random.fold_in(key, 12), (N_ROW, N_COL), 0, ceiling // 4 + 1)
    values = ceiling - jitter
    full_cell = jax.random.randint(jax.random.fold_in(key, 13), (), 0, N_ROW * N_COL)
    cell_ids = jnp.arange(N_ROW * N_COL, dtype=jnp.int32).reshape(N_ROW, N_COL)
    return jnp.where(cell_ids == full_cell, SLOTS, values).astype(jnp.int32)


def block_scale(rng, extent, cuts, low, top_value):
    factor_of = 1.0
    for position, blocks in cuts:
        heights = jax.random.uniform(jax.random.fold_in(jax.random.fold_in(rng, 6), position), (blocks,), jnp.float32, low / len(cuts), top_value / len(cuts))
        factor_of = factor_of * jnp.repeat(jnp.exp(heights), extent[position] // blocks).reshape((-1,) + (1,) * (len(extent) - 1 - position))
    return factor_of


def normal_values(own_key, dims, width, bound, split=(), held_as=jnp.bfloat16):
    values = jax.random.normal(own_key, dims, jnp.float32) * width
    if len(split) > 0:
        values = block_scale(own_key, dims, split, -0.22, 0.18) * values
    return jnp.clip(values, min=-bound, max=bound).astype(held_as)


def setup_inputs(seed: int = 0) -> dict:
    key_list = jax.random.split(jax.random.key(seed), 8)
    return {
        "features": normal_values(key_list[0], (NVERT, F), 1.0, 6.0, ((0, 128),)),
        "weight": normal_values(key_list[1], (F, F), F ** -0.5, 0.375),
        "adj_rows": draw_adj_rows(jax.random.fold_in(key_list[7], 71), 0),
        "adj_cols": draw_adj_cols(jax.random.fold_in(key_list[7], 71), 0),
        "adj_blocks": draw_adj_blocks(jax.random.fold_in(key_list[7], 71), 0),
        "counts": draw_counts(jax.random.fold_in(key_list[7], 71), 0),
        "grad_out": normal_values(key_list[6], (NVERT, F), 1.0, 6.0, ((0, 128),)),
    }


def cell_partial(slab, slab_rows, slab_cols, blocks, live_count):
    picked = slab.reshape(CB, BS, F)[slab_cols].astype(jnp.float32)
    live_mask = (jnp.arange(SLOTS) < live_count).astype(jnp.float32)
    products = jnp.einsum('kil,klf->kif', blocks.astype(jnp.float32), picked) * live_mask[:, None, None]
    summed = jax.ops.segment_sum(products, slab_rows, num_segments=RB)
    return summed.reshape(RB * BS, F)


def reference(features, weight, adj_rows, adj_cols, adj_blocks, counts, grad_out):
    slabs = features.reshape(N_COL, CB * BS, F)

    def one_row(slab_row):
        def add_cell(running, slab_col):
            partial_value = cell_partial(slabs[slab_col], adj_rows[slab_row, slab_col], adj_cols[slab_row, slab_col], adj_blocks[slab_row, slab_col], counts[slab_row, slab_col])
            rounded = lax.optimization_barrier(partial_value.astype(jnp.bfloat16)).astype(jnp.float32)
            return running + rounded, None

        running, _ = lax.scan(add_cell, jnp.zeros((RB * BS, F), jnp.float32), jnp.arange(N_COL))
        return running.astype(jnp.bfloat16)

    agg = lax.map(one_row, jnp.arange(N_ROW)).reshape(NVERT, F)
    preact = jnp.dot(agg, weight, preferred_element_type=jnp.float32)
    out_row = jax.nn.silu(preact).astype(jnp.bfloat16)
    out_col = out_row.reshape(DEVICES, N_ROW, N_COL, SUB, F).transpose(2, 1, 0, 3, 4).reshape(NVERT, F)
    grad_row = grad_out.reshape(N_COL, N_ROW, DEVICES, SUB, F).transpose(2, 1, 0, 3, 4).reshape(NVERT, F)
    sigmoid_pre = jax.nn.sigmoid(preact)
    grad_pre = (grad_row.astype(jnp.float32) * sigmoid_pre * (1.0 + preact * (1.0 - sigmoid_pre))).astype(jnp.bfloat16)
    weight_grad = jnp.dot(agg.T, grad_pre, preferred_element_type=jnp.float32) * (NVERT ** -0.5)
    return out_col, weight_grad
```

```python
import functools

import jax
import jax.numpy as jnp
from jax import lax
from jax.experimental import pallas as pl
from jax.experimental.pallas import tpu as pltpu
from jax.sharding import Mesh, PartitionSpec as P

BS = 128
LANES = 128
OWNER_BLOCKS = 16
TURNS = 8
PEERS = 8
Z_ORDER = (2, 1, 3, 0)


def ring(size, step):
    return [(i, (i + step) % size) for i in range(size)]


def load_slab(pieces, slab, sems):
    copies = []
    start = 0
    for n, piece in enumerate(pieces):
        rows = piece.shape[0]
        copy = pltpu.make_async_copy(piece, slab.at[pl.ds(start, rows)], sems.at[n])
        copy.start()
        copies.append(copy)
        start += rows
    for copy in copies:
        copy.wait()


def product(adj_ref, slab, cols, slot, turn):
    start = pl.multiple_of(cols[slot] * BS, BS)
    return jnp.dot(
        adj_ref[turn, 0, 0], slab[pl.ds(start, BS), :], preferred_element_type=jnp.float32
    )


def other_core_kernel(n_pieces, cols, count, owners, core, adj_ref, *refs):
    pieces, (out_ref, slab, sems) = refs[:n_pieces], refs[n_pieces:]
    step = pl.program_id(0)

    @pl.when(step == 0)
    def _():
        load_slab(pieces, slab, sems)

    for turn in range(TURNS):
        slot = turn * 16 + owners[step] * 2 + 1 - core[0]

        @pl.when(slot < count[0])
        def _():
            out_ref[0, turn] = product(adj_ref, slab, cols, slot, turn).astype(out_ref.dtype)


def own_core_kernel(
    n_pieces, cols, rows, count, other_rows, other_count, owners, core, adj_ref, other_ref, *refs
):
    pieces, outs, (slab, sums, sems) = refs[:n_pieces], refs[n_pieces:-3], refs[-3:]
    step = pl.program_id(0)

    @pl.when(step == 0)
    def _():
        load_slab(pieces, slab, sems)

    sums[...] = jnp.zeros_like(sums)
    for turn in range(TURNS):
        slot = turn * 16 + owners[step] * 2 + core[0]

        @pl.when(slot < count[0])
        def _():
            sums[rows[slot]] = product(adj_ref, slab, cols, slot, turn).astype(sums.dtype)

    for turn in range(TURNS):
        slot = turn * 16 + owners[step] * 2 + core[0]

        @pl.when(slot < other_count[0])
        def _():
            row = other_rows[slot]
            total = sums[row].astype(jnp.float32) + other_ref[0, turn].astype(jnp.float32)
            sums[row] = total.astype(sums.dtype)

    half = OWNER_BLOCKS // 2
    for place in range(len(Z_ORDER)):

        @pl.when(step // 2 == place)
        def _():
            outs[2 * place][0] = sums[:half]
            outs[2 * place + 1][0] = sums[half:]


def slab_products(pieces, tables, adj):
    cols, rows, count, other_rows, other_count, owners, core = tables
    slab_rows = sum(piece.shape[0] for piece in pieces)
    n_pieces = len(pieces)
    any_spec = pl.BlockSpec(memory_space=pl.ANY)
    slab_scratch = pltpu.VMEM((slab_rows, LANES), jnp.bfloat16)
    sems = pltpu.SemaphoreType.DMA((n_pieces,))
    params = pltpu.CompilerParams(
        dimension_semantics=("arbitrary",), vmem_limit_bytes=32 * 1024 * 1024
    )
    cost = pl.CostEstimate(
        flops=2 * 64 * BS * BS * LANES, bytes_accessed=10 * 1024 * 1024, transcendentals=0
    )
    adj_block = (TURNS, 1, 1, BS, BS)
    other = pl.pallas_call(
        functools.partial(other_core_kernel, n_pieces),
        out_shape=jax.ShapeDtypeStruct((PEERS, TURNS, BS, LANES), jnp.bfloat16),
        grid_spec=pltpu.PrefetchScalarGridSpec(
            num_scalar_prefetch=4,
            grid=(PEERS,),
            in_specs=[
                pl.BlockSpec(adj_block, lambda g, cl, ct, ow, co: (0, ow[g], 1 - co[0], 0, 0)),
                *[any_spec] * n_pieces,
            ],
            out_specs=pl.BlockSpec((1, TURNS, BS, LANES), lambda g, *_: (g, 0, 0, 0)),
            scratch_shapes=[slab_scratch, sems],
        ),
        compiler_params=params,
        cost_estimate=cost,
        name="other_core",
    )(cols, count, owners, core, adj, *pieces)
    came = lax.ppermute(other, "core", ring(2, 1))
    half = OWNER_BLOCKS // 2
    out_shape, out_specs = [], []
    for place in range(len(Z_ORDER)):
        for _ in range(2):
            out_shape.append(jax.ShapeDtypeStruct((2, half, BS, LANES), jnp.bfloat16))
            out_specs.append(
                pl.BlockSpec(
                    (1, half, BS, LANES),
                    lambda g, *_, first=2 * place: (jnp.clip(g - first, 0, 1), 0, 0, 0),
                )
            )
    return pl.pallas_call(
        functools.partial(own_core_kernel, n_pieces),
        out_shape=out_shape,
        grid_spec=pltpu.PrefetchScalarGridSpec(
            num_scalar_prefetch=7,
            grid=(PEERS,),
            in_specs=[
                pl.BlockSpec(
                    adj_block, lambda g, cl, rw, ct, orw, oct, ow, co: (0, ow[g], co[0], 0, 0)
                ),
                pl.BlockSpec((1, TURNS, BS, LANES), lambda g, *_: (g, 0, 0, 0)),
                *[any_spec] * n_pieces,
            ],
            out_specs=out_specs,
            scratch_shapes=[
                slab_scratch,
                pltpu.VMEM((OWNER_BLOCKS, BS, LANES), jnp.bfloat16),
                sems,
            ],
        ),
        compiler_params=params,
        cost_estimate=cost,
        name="own_core",
    )(cols, rows, count, other_rows, other_count, owners, core, adj, came, *pieces)


def gather_first(own):
    up = lax.ppermute(own, "y", ring(4, 1))
    down = lax.ppermute(own, "y", ring(4, -1))
    side = lax.ppermute(own, "xl", ring(2, 1))
    return up, down, side


def gather_second(up, down, side):
    half = up.shape[0] // 2
    far_low = lax.ppermute(up[:half], "y", ring(4, 1))
    far_high = lax.ppermute(down[half:], "y", ring(4, -1))
    side_up = lax.ppermute(side, "y", ring(4, 1))
    side_down = lax.ppermute(side, "y", ring(4, -1))
    return far_low, far_high, side_up, side_down


def gather_third(side_up, side_down):
    half = side_up.shape[0] // 2
    return (
        lax.ppermute(side_up[:half], "y", ring(4, 1)),
        lax.ppermute(side_down[half:], "y", ring(4, -1)),
    )


def add(*terms):
    total = terms[0].astype(jnp.float32)
    for term in terms[1:]:
        total = total + term.astype(jnp.float32)
    return total.astype(jnp.bfloat16)


def reduce_to_owner(parts):
    far_low, far_high, next_low, next_high, prev_low, prev_high, own_low, own_high = parts
    up, down = ring(4, 1), ring(4, -1)
    via_low = lax.ppermute(far_low, "z", up)
    via_high = lax.ppermute(far_high, "z", down)
    got_high_1 = lax.ppermute(next_high, "z", up)
    got_low_1 = lax.ppermute(prev_low, "z", down)
    got_low_2 = lax.ppermute(add(next_low, via_low), "z", up)
    got_high_2 = lax.ppermute(add(prev_high, via_high), "z", down)
    side_low = lax.ppermute(add(own_low[1], got_low_1[1], got_low_2[1]), "xh", ring(2, 1))
    side_high = lax.ppermute(add(own_high[1], got_high_1[1], got_high_2[1]), "xh", ring(2, 1))
    low = add(own_low[0], got_low_1[0], got_low_2[0], side_low)
    high = add(own_high[0], got_high_1[0], got_high_2[0], side_high)
    return jnp.concatenate([low, high]).reshape(-1, LANES)


def derivative(preact, grad_rows):
    sigmoid_pre = jax.nn.sigmoid(preact)
    return (
        grad_rows.astype(jnp.float32) * sigmoid_pre * (1.0 + preact * (1.0 - sigmoid_pre))
    ).astype(jnp.bfloat16)


AXES = ("xl", "y", "xh", "z", "core")


def swap_all(rows, devices_all):
    return lax.all_to_all(
        rows.reshape(devices_all, -1, rows.shape[-1]), AXES, split_axis=0, concat_axis=0, tiled=True
    )


def on_device(features, weight, adj_rows, adj_cols, adj_blocks, counts, grad_out):
    local_rows, feat_width = features.shape
    devices_all = 128
    xl, y, xh, z, core = (lax.axis_index(name) for name in AXES)

    count = counts.reshape(1)
    slots = jnp.arange(adj_rows.shape[-1], dtype=jnp.int32)
    rows = adj_rows.reshape(-1) - (slots % 16) * OWNER_BLOCKS
    other_rows = lax.ppermute(rows, "core", ring(2, 1))
    other_count = lax.ppermute(count, "core", ring(2, 1))
    cols = adj_cols.reshape(-1)
    source = cols // OWNER_BLOCKS
    away = ((source // 4) ^ xl) * 4 + (source % 4 - y) % 4
    cols = away * OWNER_BLOCKS + cols % OWNER_BLOCKS
    owners = jnp.stack([(xh ^ dx) * 4 + (z + dz) % 4 for dz in Z_ORDER for dx in range(2)])
    tables = (cols, rows, count, other_rows, other_count, owners.astype(jnp.int32), core.reshape(1))
    adj = adj_blocks.reshape(TURNS, PEERS, 2, BS, BS)

    aggs = []
    after = None
    for part in range(feat_width // LANES):
        own = features[:, part * LANES : (part + 1) * LANES]
        if after is not None:
            own, _ = lax.optimization_barrier((own, after))
        up, down, side = gather_first(own)
        far_low, far_high, side_up, side_down = gather_second(up, down, side)
        after = (far_low, side_up)
        side_far_low, side_far_high = gather_third(side_up, side_down)
        pieces = (
            own, down, far_low, far_high, up,
            side, side_down, side_far_low, side_far_high, side_up,
        )
        aggs.append(reduce_to_owner(slab_products(pieces, tables, adj)))
    agg = jnp.concatenate(aggs, axis=1)

    grad_row = swap_all(grad_out, devices_all).reshape(local_rows, feat_width)
    preact = jnp.dot(agg, weight, preferred_element_type=jnp.float32)
    out_row = jax.nn.silu(preact).astype(jnp.bfloat16)
    out_col = swap_all(out_row, devices_all).reshape(local_rows, feat_width)
    grad_pre = derivative(preact, grad_row)
    contract = (((0,), (0,)), ((), ()))
    weight_part = lax.dot_general(agg, grad_pre, contract, preferred_element_type=jnp.float32)
    terms = swap_all(weight_part, devices_all)
    summed = jnp.sum(terms, axis=0) * (local_rows * devices_all) ** (-0.5)
    spread = jnp.broadcast_to(summed[None], (devices_all, *summed.shape))
    weight_grad = lax.all_to_all(spread, AXES, split_axis=0, concat_axis=0, tiled=True)
    return (out_col, weight_grad.reshape(feat_width, feat_width))


def solution(mesh):
    fine = Mesh(mesh.devices.reshape(2, 4, 2, 4, 2), AXES)
    row, col = ("xl", "y"), ("xh", "z", "core")
    placed = (
        P((*col, *row), None),
        P(),
        P(row, col, None),
        P(row, col, None),
        P(row, col, None, None, None),
        P(row, col),
        P((*col, *row), None),
    )
    return jax.shard_map(
        on_device,
        mesh=fine,
        in_specs=placed,
        out_specs=(P((*col, *row), None), P()),
        check_vma=False,
    )
```

```python
import functools

import jax
import jax.numpy as jnp
from jax import lax
from jax.experimental import pallas as pl
from jax.experimental.pallas import tpu as pltpu
from jax.sharding import Mesh, PartitionSpec as P

BS = 128
LANES = 128
OWNER_BLOCKS = 16
TURNS = 8
PEERS = 8
Z_ORDER = (2, 1, 3, 0)


def ring(size, step):
    return [(i, (i + step) % size) for i in range(size)]


def load_slab(pieces, slab, sems):
    copies = []
    start = 0
    for n, piece in enumerate(pieces):
        rows = piece.shape[0]
        copy = pltpu.make_async_copy(piece, slab.at[pl.ds(start, rows)], sems.at[n])
        copy.start()
        copies.append(copy)
        start += rows
    for copy in copies:
        copy.wait()


def chip_kernel(n_pieces, tables, owners, core, adj_ref, other_adj_ref, *refs):
    pieces, outs, (slab, sums, sems) = refs[:n_pieces], refs[n_pieces:-3], refs[-3:]
    step = pl.program_id(0)

    @pl.when(step == 0)
    def _():
        load_slab(pieces, slab, sems)

    sums[...] = jnp.zeros_like(sums)

    def product(cell, slot, block):
        start = pl.multiple_of(tables[cell, 0, slot] * BS, BS)
        found = jnp.dot(block, slab[pl.ds(start, BS), :], preferred_element_type=jnp.float32)
        return jnp.where(slot < tables[cell, 2, 0], found, 0.0).astype(jnp.bfloat16)

    slots = [turn * 16 + owners[step] * 2 + core[0] for turn in range(TURNS)]
    for turn, slot in enumerate(slots):
        sums[tables[0, 1, slot]] = product(0, slot, adj_ref[turn, 0, 0])
    for turn, slot in enumerate(slots):
        row = tables[1, 1, slot]
        term = product(1, slot, other_adj_ref[turn, 0]).astype(jnp.float32)
        sums[row] = (sums[row].astype(jnp.float32) + term).astype(jnp.bfloat16)

    half = OWNER_BLOCKS // 2
    for place in range(len(Z_ORDER)):

        @pl.when(step // 2 == place)
        def _():
            outs[2 * place][0] = sums[:half]
            outs[2 * place + 1][0] = sums[half:]


def chip_sums(pieces, tables, owners, core, adj, other_adj):
    slab_rows = sum(piece.shape[0] for piece in pieces)
    n_pieces = len(pieces)
    half = OWNER_BLOCKS // 2
    out_shape, out_specs = [], []
    for place in range(len(Z_ORDER)):
        for _ in range(2):
            out_shape.append(jax.ShapeDtypeStruct((2, half, BS, LANES), jnp.bfloat16))
            out_specs.append(
                pl.BlockSpec(
                    (1, half, BS, LANES),
                    lambda g, *_, first=2 * place: (jnp.clip(g - first, 0, 1), 0, 0, 0),
                )
            )
    return pl.pallas_call(
        functools.partial(chip_kernel, n_pieces),
        out_shape=out_shape,
        grid_spec=pltpu.PrefetchScalarGridSpec(
            num_scalar_prefetch=3,
            grid=(PEERS,),
            in_specs=[
                pl.BlockSpec((TURNS, 1, 1, BS, BS), lambda g, tb, ow, co: (0, ow[g], co[0], 0, 0)),
                pl.BlockSpec((TURNS, 1, BS, BS), lambda g, tb, ow, co: (0, ow[g], 0, 0)),
                *[pl.BlockSpec(memory_space=pl.ANY)] * n_pieces,
            ],
            out_specs=out_specs,
            scratch_shapes=[
                pltpu.VMEM((slab_rows, LANES), jnp.bfloat16),
                pltpu.VMEM((OWNER_BLOCKS, BS, LANES), jnp.bfloat16),
                pltpu.SemaphoreType.DMA((n_pieces,)),
            ],
        ),
        compiler_params=pltpu.CompilerParams(
            dimension_semantics=("arbitrary",), vmem_limit_bytes=32 * 1024 * 1024
        ),
        cost_estimate=pl.CostEstimate(
            flops=12_000_000_000, bytes_accessed=16 * 1024 * 1024, transcendentals=0
        ),
        name="chip_sums",
    )(tables, owners, core, adj, other_adj, *pieces)


def gather_first(own):
    up = lax.ppermute(own, "y", ring(4, 1))
    down = lax.ppermute(own, "y", ring(4, -1))
    side = lax.ppermute(own, "xl", ring(2, 1))
    return up, down, side


def gather_second(up, down, side):
    half = up.shape[0] // 2
    far_low = lax.ppermute(up[:half], "y", ring(4, 1))
    far_high = lax.ppermute(down[half:], "y", ring(4, -1))
    side_up = lax.ppermute(side, "y", ring(4, 1))
    side_down = lax.ppermute(side, "y", ring(4, -1))
    return far_low, far_high, side_up, side_down


def gather_third(side_up, side_down):
    half = side_up.shape[0] // 2
    return (
        lax.ppermute(side_up[:half], "y", ring(4, 1)),
        lax.ppermute(side_down[half:], "y", ring(4, -1)),
    )


def add(*terms):
    total = terms[0].astype(jnp.float32)
    for term in terms[1:]:
        total = total + term.astype(jnp.float32)
    return total.astype(jnp.bfloat16)


def reduce_to_owner(parts):
    far_low, far_high, next_low, next_high, prev_low, prev_high, own_low, own_high = parts
    up, down = ring(4, 1), ring(4, -1)
    via_low = lax.ppermute(far_low, "z", up)
    via_high = lax.ppermute(far_high, "z", down)
    got_high_1 = lax.ppermute(next_high, "z", up)
    got_low_1 = lax.ppermute(prev_low, "z", down)
    got_low_2 = lax.ppermute(add(next_low, via_low), "z", up)
    got_high_2 = lax.ppermute(add(prev_high, via_high), "z", down)
    side_low = lax.ppermute(add(own_low[1], got_low_1[1], got_low_2[1]), "xh", ring(2, 1))
    side_high = lax.ppermute(add(own_high[1], got_high_1[1], got_high_2[1]), "xh", ring(2, 1))
    low = add(own_low[0], got_low_1[0], got_low_2[0], side_low)
    high = add(own_high[0], got_high_1[0], got_high_2[0], side_high)
    return jnp.concatenate([low, high]).reshape(-1, LANES)


def derivative(preact, grad_rows):
    sigmoid_pre = jax.nn.sigmoid(preact)
    return (
        grad_rows.astype(jnp.float32) * sigmoid_pre * (1.0 + preact * (1.0 - sigmoid_pre))
    ).astype(jnp.bfloat16)


AXES = ("xl", "y", "xh", "z", "core")


def swap_all(rows, devices_all):
    return lax.all_to_all(
        rows.reshape(devices_all, -1, rows.shape[-1]), AXES, split_axis=0, concat_axis=0, tiled=True
    )


def on_device(features, weight, adj_rows, adj_cols, adj_blocks, counts, grad_out):
    local_rows, feat_width = features.shape
    devices_all = 128
    xl, y, xh, z, core = (lax.axis_index(name) for name in AXES)
    swap_core = functools.partial(lax.ppermute, axis_name="core", perm=ring(2, 1))

    slots = jnp.arange(adj_rows.shape[-1], dtype=jnp.int32)
    rows = adj_rows.reshape(-1) - (slots % 16) * OWNER_BLOCKS
    cols = adj_cols.reshape(-1)
    source = cols // OWNER_BLOCKS
    away = ((source // 4) ^ xl) * 4 + (source % 4 - y) % 4
    cols = away * OWNER_BLOCKS + cols % OWNER_BLOCKS
    mine = jnp.stack([cols, rows, jnp.broadcast_to(counts.reshape(1), rows.shape)])
    theirs = swap_core(mine).at[0].add(slots.shape[0])
    tables = jnp.stack([mine, theirs])
    owners = jnp.stack([(xh ^ dx) * 4 + (z + dz) % 4 for dz in Z_ORDER for dx in range(2)])
    owners = owners.astype(jnp.int32)
    adj = adj_blocks.reshape(TURNS, PEERS, 2, BS, BS)
    other_adj = swap_core(lax.dynamic_index_in_dim(adj, 1 - core, 2, keepdims=False))

    aggs = []
    after = None
    for part in range(feat_width // LANES):
        own = features[:, part * LANES : (part + 1) * LANES]
        if after is not None:
            own, _ = lax.optimization_barrier((own, after))
        up, down, side = gather_first(own)
        if part == 0:
            grad_out, _ = lax.optimization_barrier((grad_out, up))
            grad_row = swap_all(grad_out, devices_all).reshape(local_rows, feat_width)
        far_low, far_high, side_up, side_down = gather_second(up, down, side)
        after = (far_low, side_up)
        side_far_low, side_far_high = gather_third(side_up, side_down)
        pieces = (
            own, down, far_low, far_high, up,
            side, side_down, side_far_low, side_far_high, side_up,
        )
        pieces = (*pieces, *[swap_core(piece) for piece in pieces])
        if part == 0:
            tables, grad_row = lax.optimization_barrier((tables, grad_row))
        parts = chip_sums(pieces, tables, owners, core.reshape(1), adj, other_adj)
        aggs.append(reduce_to_owner(parts))
    agg = jnp.concatenate(aggs, axis=1)

    preact = jnp.dot(agg, weight, preferred_element_type=jnp.float32)
    out_row = jax.nn.silu(preact).astype(jnp.bfloat16)
    grad_pre = derivative(preact, grad_row)
    contract = (((0,), (0,)), ((), ()))
    weight_part = lax.dot_general(agg, grad_pre, contract, preferred_element_type=jnp.float32)
    coarse = lax.reduce_precision(weight_part, 8, 7)
    terms = [coarse.astype(jnp.bfloat16), (weight_part - coarse).astype(jnp.bfloat16)]
    sent = jnp.concatenate([x.reshape(devices_all, -1, feat_width) for x in (out_row, *terms)], 1)
    came = lax.all_to_all(sent, AXES, split_axis=0, concat_axis=0, tiled=True)
    piece = local_rows // devices_all
    out_col = came[:, :piece].reshape(local_rows, feat_width)
    came = came[:, piece:].astype(jnp.float32)
    each = came.shape[1] // 2
    summed = jnp.sum(came[:, :each] + came[:, each:], axis=0) * (local_rows * devices_all) ** (-0.5)
    spread = jnp.broadcast_to(summed[None], (devices_all, *summed.shape))
    weight_grad = lax.all_to_all(spread, AXES, split_axis=0, concat_axis=0, tiled=True)
    return (out_col, weight_grad.reshape(feat_width, feat_width))


def solution(mesh):
    fine = Mesh(mesh.devices.reshape(2, 4, 2, 4, 2), AXES)
    row, col = ("xl", "y"), ("xh", "z", "core")
    placed = (
        P((*col, *row), None),
        P(),
        P(row, col, None),
        P(row, col, None),
        P(row, col, None, None, None),
        P(row, col),
        P((*col, *row), None),
    )
    return jax.shard_map(
        on_device,
        mesh=fine,
        in_specs=placed,
        out_specs=(P((*col, *row), None), P()),
        check_vma=False,
    )
```

```python
import functools

import jax
import jax.numpy as jnp
from jax import lax
from jax.experimental import pallas as pl
from jax.experimental.pallas import tpu as pltpu
from jax.sharding import Mesh, PartitionSpec as P

BS = 128
WIDTH = 256
OWNER_BLOCKS = 16
LOW = 9
SIDE_FIRST = 10
TURNS = 8
PEERS = 8
CB = 128


def ring(size, step):
    return [(i, (i + step) % size) for i in range(size)]


def permute(value, axis, step):
    return lax.ppermute(value, axis, ring(lax.axis_size(axis), step))


def load_slab(layout, pieces, slab, sems):
    copies = []
    for n, (piece, start, rows, place) in enumerate(layout):
        source = pieces[piece].at[pl.ds(start, rows)]
        copy = pltpu.make_async_copy(source, slab.at[pl.ds(place, rows)], sems.at[n])
        copy.start()
        copies.append(copy)
    for copy in copies:
        copy.wait()


def chip_kernel(
    layout, n_pieces, stores, tables, owners, core, adj_ref, other_adj_ref, *refs
):
    pieces, outs, (slab, sums, sems) = refs[:n_pieces], refs[n_pieces:-3], refs[-3:]
    step = pl.program_id(0)

    @pl.when(step == 0)
    def _():
        load_slab(layout, pieces, slab, sems)

    sums[...] = jnp.zeros_like(sums)

    def product(cell, slot, block):
        start = pl.multiple_of(tables[cell, 0, slot] * BS, BS)
        found = jnp.dot(block, slab[pl.ds(start, BS), :], preferred_element_type=jnp.float32)
        return jnp.where(slot < tables[cell, 2, 0], found, 0.0).astype(jnp.bfloat16)

    slots = [turn * 16 + owners[step] * 2 + core[0] for turn in range(TURNS)]
    for turn, slot in enumerate(slots):
        sums[tables[0, 1, slot]] = product(0, slot, adj_ref[turn, 0, 0])
    for turn, slot in enumerate(slots):
        row = tables[1, 1, slot]
        term = product(1, slot, other_adj_ref[turn, 0]).astype(jnp.float32)
        sums[row] = (sums[row].astype(jnp.float32) + term).astype(jnp.bfloat16)

    for out, (first, last, start, stop, every) in zip(outs, stores):

        @pl.when((step >= first) & (step < last) & ((step - first) % every == 0))
        def _():
            out[0] = sums[start:stop]


def chip_sums(gathered, distances, tables, owners, core, adj, other_adj):
    layout, pieces = gathered
    steps = 2 * len(distances)
    high = OWNER_BLOCKS - LOW
    shapes, specs, stores = [], [], []

    def output(count, blocks, place, store):
        shapes.append(jax.ShapeDtypeStruct((count, blocks, BS, WIDTH), jnp.bfloat16))
        specs.append(pl.BlockSpec((1, blocks, BS, WIDTH), lambda g, *_: (place(g), 0, 0, 0)))
        stores.append(store)

    for n, distance in enumerate(distances):
        cuts = (0, LOW // 2, LOW) if distance == 2 else (0, LOW)
        for start, stop in zip(cuts, cuts[1:]):
            output(
                2,
                stop - start,
                lambda g, first=2 * n: jnp.clip(g - first, 0, 1),
                (2 * n, 2 * n + 2, start, stop, 1),
            )
    for side in range(2):
        output(len(distances), high, lambda g: g // 2, (side, steps, LOW, OWNER_BLOCKS, 2))
    return pl.pallas_call(
        functools.partial(chip_kernel, layout, len(pieces), stores),
        out_shape=shapes,
        grid_spec=pltpu.PrefetchScalarGridSpec(
            num_scalar_prefetch=3,
            grid=(steps,),
            in_specs=[
                pl.BlockSpec((TURNS, 1, 1, BS, BS), lambda g, tb, ow, co: (0, ow[g], co[0], 0, 0)),
                pl.BlockSpec((TURNS, 1, BS, BS), lambda g, tb, ow, co: (0, ow[g], 0, 0)),
                *[pl.BlockSpec(memory_space=pl.ANY)] * len(pieces),
            ],
            out_specs=specs,
            scratch_shapes=[
                pltpu.VMEM((2 * CB * BS, WIDTH), jnp.bfloat16),
                pltpu.VMEM((OWNER_BLOCKS, BS, WIDTH), jnp.bfloat16),
                pltpu.SemaphoreType.DMA((len(layout),)),
            ],
        ),
        compiler_params=pltpu.CompilerParams(
            dimension_semantics=("arbitrary",), vmem_limit_bytes=60 * 1024 * 1024
        ),
        cost_estimate=pl.CostEstimate(
            flops=2_000_000_000 * (3 + steps), bytes_accessed=1024, transcendentals=0
        ),
        name="chip_sums",
    )(tables, owners(distances), core, adj, other_adj, *pieces)


def copy_rows_kernel(plans, n_sources, *refs):
    n_outs = len(plans)
    sources, outs, held = refs[:n_sources], refs[n_sources:-n_outs - 1], refs[-n_outs - 1 : -1]
    sems = refs[-1]
    loads, stores = [], []
    for out, buffer, plan in zip(outs, held, plans):
        place = 0
        for source, start, stop in plan:
            here, n = pl.ds(place, stop - start), len(loads)
            there = sources[source].at[pl.ds(start, stop - start)]
            loads.append(pltpu.make_async_copy(there, buffer.at[here], sems.at[0, n]))
            stores.append(pltpu.make_async_copy(buffer.at[here], out.at[here], sems.at[1, n]))
            place += stop - start
    for load in loads:
        load.start()
    for load, store in zip(loads, stores):
        load.wait()
        store.start()
    for store in stores:
        store.wait()


def copy_rows(sources, *plans):
    sizes = [(sum(stop - start for _, start, stop in plan), WIDTH) for plan in plans]
    dtype = sources[0].dtype
    any_spec = pl.BlockSpec(memory_space=pl.ANY)
    return pl.pallas_call(
        functools.partial(copy_rows_kernel, plans, len(sources)),
        out_shape=[jax.ShapeDtypeStruct(size, dtype) for size in sizes],
        in_specs=[any_spec] * len(sources),
        out_specs=[any_spec] * len(plans),
        scratch_shapes=[
            *[pltpu.VMEM(size, dtype) for size in sizes],
            pltpu.SemaphoreType.DMA((2, sum(len(plan) for plan in plans))),
        ],
        compiler_params=pltpu.CompilerParams(vmem_limit_bytes=60 * 1024 * 1024),
        name="copy_rows",
    )(*sources)


def together(*values):
    return lax.optimization_barrier(values)


def gather(own, shared, others):
    n = own.shape[0]
    half, first = n // 2, SIDE_FIRST * BS
    last, cut = n - first, SIDE_FIRST // 2 * BS
    up, down, side = permute(own, "y", 1), permute(own, "y", -1), permute(own, "xl", 1)
    shared = [permute(value, "core", 1) for value in shared]
    up, down, side, shared = together(up, down, side, shared)
    go_up, go_down, go_across = copy_rows(
        (up, down, side),
        ((0, 0, half), (2, 0, first)),
        ((1, half, n), (2, 0, first)),
        ((0, first, n), (1, first, n)),
    )
    via_up, via_down = permute(go_up, "y", 1), permute(go_down, "y", -1)
    across = permute(go_across, "xl", 1)
    others = others(up)
    via_up, via_down, across, others = together(via_up, via_down, across, others)
    ends = copy_rows(
        (via_up, via_down),
        ((0, half, half + cut),),
        ((1, half + cut, half + first),),
        ((1, first - half, half),),
    )
    end_up = permute(ends[0], "y", 1)
    end_down = permute(ends[1], "y", -1)
    end_across = permute(ends[2], "xl", 1)
    early = [own, up, down, side, via_up, via_down, across]
    late = [end_up, end_down, end_across]
    parts = [
        [(0, n, 0)],
        [(0, n, 3 * n)],
        [(0, n, n)],
        [(0, n, 4 * n)],
        [(0, half, 2 * n), (half, first, 7 * n)],
        [(0, half, 2 * n + half), (half, first, 5 * n)],
        [(0, last, 7 * n + first), (last, last, 5 * n + first)],
        [(0, cut, 6 * n)],
        [(0, first - cut, 6 * n + cut)],
        [(0, last, 6 * n + first)],
    ]
    pieces = early + late
    pieces += [permute(x, "core", 1) for x in pieces]
    layout = [(i, *part) for i, each in enumerate(parts) for part in each]
    layout += [(len(parts) + i, start, rows, place + 8 * n) for i, start, rows, place in layout]
    return layout, pieces, shared, others


def add(*terms):
    total = terms[0].astype(jnp.float32)
    for term in terms[1:]:
        total = total + term.astype(jnp.float32)
    return total.astype(jnp.bfloat16)


def reduce_to_owner(far, near):
    far_a, far_b, keep, give = far
    via_a = permute(far_a, "z", 1)
    via_b = permute(far_b, "z", -1)
    came = permute(give, "xh", 1)
    via_a, via_b, came, near = together(via_a, via_b, came, near)
    cut = came.shape[1] // 2
    high_a = permute(add(keep[0, :cut], came[0, :cut]), "z", 1)
    high_b = permute(add(keep[0, cut:], came[0, cut:]), "z", -1)
    up, down, own, keep, give = near
    part = via_a.shape[1]
    up = lax.dynamic_update_slice(up, add(up[:, :part], via_a), (0, 0, 0, 0))
    down = lax.dynamic_update_slice(down, add(down[:, part:], via_b), (0, part, 0, 0))
    came = permute(give, "xh", 1)
    up, down, came, high_a, high_b = together(
        permute(up, "z", 1), permute(down, "z", -1), came, high_a, high_b
    )
    low_side = permute(add(own[1], up[1], down[1]), "xh", 1)
    high = [add(keep[n], came[n]) for n in range(2)]
    high_up = jnp.concatenate([add(high[0][:cut], high_a), high[0][cut:]])
    high_down = jnp.concatenate([high[1][:cut], add(high[1][cut:], high_b)])
    low_side, high_up, high_down = together(
        low_side, permute(high_up, "z", 1), permute(high_down, "z", -1)
    )
    high = add(keep[2], came[2], high_up, high_down)
    return jnp.concatenate([add(own[0], up[0], down[0], low_side), high]).reshape(-1, WIDTH)


def derivative(preact, grad_rows):
    sigmoid_pre = jax.nn.sigmoid(preact)
    return (
        grad_rows.astype(jnp.float32) * sigmoid_pre * (1.0 + preact * (1.0 - sigmoid_pre))
    ).astype(jnp.bfloat16)


AXES = ("xl", "y", "xh", "z", "core")


def swap_all(rows, devices_all):
    return lax.all_to_all(
        rows.reshape(devices_all, -1, rows.shape[-1]), AXES, split_axis=0, concat_axis=0, tiled=True
    )


def on_device(features, weight, adj_rows, adj_cols, adj_blocks, counts, grad_out):
    local_rows, feat_width = features.shape
    devices_all = 128
    xl, y, xh, z, core = (lax.axis_index(name) for name in AXES)

    slots = jnp.arange(adj_rows.shape[-1], dtype=jnp.int32)
    rows = adj_rows.reshape(-1) - (slots % 16) * OWNER_BLOCKS
    cols = adj_cols.reshape(-1)
    source = cols // OWNER_BLOCKS
    away = ((source // 4) ^ xl) * 4 + (source % 4 - y) % 4
    cols = away * OWNER_BLOCKS + cols % OWNER_BLOCKS
    mine = jnp.stack([cols, rows, jnp.broadcast_to(counts.reshape(1), rows.shape)])

    def owners(distances):
        chips = [(xh ^ dx) * 4 + (z + dz) % 4 for dz in distances for dx in range(2)]
        return jnp.stack(chips).astype(jnp.int32)

    adj = adj_blocks.reshape(TURNS, PEERS, 2, BS, BS)
    other_adj = lax.dynamic_index_in_dim(adj, 1 - core, 2, keepdims=False)

    def tied(value, *others):
        return lax.optimization_barrier((value, others))[0]

    sub_rows = local_rows // devices_all

    def grads_first(after):
        grads = tied(grad_out, after).reshape(2, 4, 16, sub_rows, feat_width)
        grads = grads.transpose(0, 2, 1, 3, 4).reshape(32, 4, sub_rows, feat_width)
        return lax.all_to_all(grads, ("xl", "xh", "z", "core"), 0, 0, tiled=True)

    def grads_last(grads, after):
        grads = tied(grads, after).transpose(1, 0, 2, 3)
        grads = lax.all_to_all(grads, "y", 0, 0, tiled=True)
        grads = grads.reshape(4, 2, 16, sub_rows, feat_width).transpose(1, 0, 2, 3, 4)
        return grads.reshape(local_rows, feat_width)

    layout, pieces, (theirs, other_adj), grads = gather(features, (mine, other_adj), grads_first)
    tables = jnp.stack([mine, theirs.at[0].add(CB)])
    products = functools.partial(
        chip_sums, tables=tables, owners=owners, core=core.reshape(1), adj=adj, other_adj=other_adj
    )
    far = products((layout, pieces), (2,))

    near = products((layout, pieces), (1, 3, 0))
    agg = reduce_to_owner(far, near)
    grad_row = grads_last(grads, near)

    preact = jnp.dot(agg, weight, preferred_element_type=jnp.float32)
    out_row = jax.nn.silu(preact).astype(jnp.bfloat16)
    grad_pre = derivative(preact, grad_row)
    contract = (((0,), (0,)), ((), ()))
    weight_part = lax.dot_general(agg, grad_pre, contract, preferred_element_type=jnp.float32)
    coarse = lax.reduce_precision(weight_part, 8, 7)
    terms = [coarse.astype(jnp.bfloat16), (weight_part - coarse).astype(jnp.bfloat16)]
    lanes = [out_row[:, :BS], out_row[:, BS:], *terms]
    sent = jnp.concatenate([x.reshape(devices_all, -1, BS) for x in lanes], axis=1)
    came = lax.all_to_all(sent, AXES, split_axis=0, concat_axis=0, tiled=True)
    piece = local_rows // devices_all
    out_col = jnp.concatenate([came[:, :piece], came[:, piece : 2 * piece]], axis=2)
    out_col = out_col.reshape(local_rows, feat_width)
    came = came[:, 2 * piece :].astype(jnp.float32)
    each = came.shape[1] // 2
    summed = jnp.sum(came[:, :each] + came[:, each:], axis=0) * (local_rows * devices_all) ** (-0.5)
    summed = summed.reshape(-1, feat_width)
    spread = jnp.broadcast_to(summed[None], (devices_all, *summed.shape))
    weight_grad = lax.all_to_all(spread, AXES, split_axis=0, concat_axis=0, tiled=True)
    return (out_col, weight_grad.reshape(feat_width, feat_width))


def solution(mesh):
    fine = Mesh(mesh.devices.reshape(2, 4, 2, 4, 2), AXES)
    row, col = ("xl", "y"), ("xh", "z", "core")
    placed = (
        P((*col, *row), None),
        P(),
        P(row, col, None),
        P(row, col, None),
        P(row, col, None, None, None),
        P(row, col),
        P((*col, *row), None),
    )
    return jax.shard_map(
        on_device,
        mesh=fine,
        in_specs=placed,
        out_specs=(P((*col, *row), None), P()),
        check_vma=False,
    )
```

```python
import functools

import jax
import jax.numpy as jnp
from jax import lax
from jax.experimental import pallas as pl
from jax.experimental.pallas import tpu as pltpu
from jax.sharding import Mesh, PartitionSpec as P

BS = 128
WIDTH = 256
OWNER_BLOCKS = 16
LOW = 8
SIDE_FIRST = 10
TURNS = 8
PEERS = 8
CB = 128


def ring(size, step):
    return [(i, (i + step) % size) for i in range(size)]


def permute(value, axis, step):
    return lax.ppermute(value, axis, ring(lax.axis_size(axis), step))


def slab_copies(layout, pieces, slab, sems):
    return [
        pltpu.make_async_copy(
            pieces[piece].at[pl.ds(start, rows)], slab.at[pl.ds(place, rows)], sems.at[n]
        )
        for n, (piece, start, rows, place) in enumerate(layout)
    ]


def chip_kernel(
    layout, n_pieces, stores, tables, owners, core, adj_ref, other_adj_ref, *refs
):
    pieces, outs, (slab, sums, sems) = refs[:n_pieces], refs[n_pieces:-3], refs[-3:]
    step = pl.program_id(0)

    @pl.when(step == 0)
    def _():
        for copy in slab_copies(layout, pieces, slab, sems):
            copy.start()
        for copy in slab_copies(layout, pieces, slab, sems)[: len(layout) // 2]:
            copy.wait()

    sums[...] = jnp.zeros_like(sums)

    def product(cell, slot, block):
        start = pl.multiple_of(tables[cell, 0, slot] * BS, BS)
        found = jnp.dot(block, slab[pl.ds(start, BS), :], preferred_element_type=jnp.float32)
        return jnp.where(slot < tables[cell, 2, 0], found, 0.0).astype(jnp.bfloat16)

    slots = [turn * 16 + owners[step] * 2 + core[0] for turn in range(TURNS)]
    for turn, slot in enumerate(slots):
        sums[tables[0, 1, slot]] = product(0, slot, adj_ref[turn, 0, 0])

    @pl.when(step == 0)
    def _():
        for copy in slab_copies(layout, pieces, slab, sems)[len(layout) // 2 :]:
            copy.wait()

    for turn, slot in enumerate(slots):
        row = tables[1, 1, slot]
        term = product(1, slot, other_adj_ref[turn, 0]).astype(jnp.float32)
        sums[row] = (sums[row].astype(jnp.float32) + term).astype(jnp.bfloat16)

    for out, (first, last, start, stop, every) in zip(outs, stores):

        @pl.when((step >= first) & (step < last) & ((step - first) % every == 0))
        def _():
            out[0] = sums[start:stop]


def chip_sums(gathered, distances, tables, owners, core, adj, other_adj):
    layout, pieces = gathered
    steps = 2 * len(distances)
    high = OWNER_BLOCKS - LOW
    shapes, specs, stores = [], [], []

    def output(count, blocks, place, store):
        shapes.append(jax.ShapeDtypeStruct((count, blocks, BS, WIDTH), jnp.bfloat16))
        specs.append(pl.BlockSpec((1, blocks, BS, WIDTH), lambda g, *_: (place(g), 0, 0, 0)))
        stores.append(store)

    for n, distance in enumerate(distances):
        cuts = (0, LOW // 2, LOW) if distance == 2 else (0, LOW)
        for start, stop in zip(cuts, cuts[1:]):
            output(
                2,
                stop - start,
                lambda g, first=2 * n: jnp.clip(g - first, 0, 1),
                (2 * n, 2 * n + 2, start, stop, 1),
            )
    for side in range(2):
        output(len(distances), high, lambda g: g // 2, (side, steps, LOW, OWNER_BLOCKS, 2))
    return pl.pallas_call(
        functools.partial(chip_kernel, layout, len(pieces), stores),
        out_shape=shapes,
        grid_spec=pltpu.PrefetchScalarGridSpec(
            num_scalar_prefetch=3,
            grid=(steps,),
            in_specs=[
                pl.BlockSpec((TURNS, 1, 1, BS, BS), lambda g, tb, ow, co: (0, ow[g], co[0], 0, 0)),
                pl.BlockSpec((TURNS, 1, BS, BS), lambda g, tb, ow, co: (0, ow[g], 0, 0)),
                *[pl.BlockSpec(memory_space=pl.ANY)] * len(pieces),
            ],
            out_specs=specs,
            scratch_shapes=[
                pltpu.VMEM((2 * CB * BS, WIDTH), jnp.bfloat16),
                pltpu.VMEM((OWNER_BLOCKS, BS, WIDTH), jnp.bfloat16),
                pltpu.SemaphoreType.DMA((len(layout),)),
            ],
        ),
        compiler_params=pltpu.CompilerParams(
            dimension_semantics=("arbitrary",), vmem_limit_bytes=60 * 1024 * 1024
        ),
        cost_estimate=pl.CostEstimate(
            flops=2_000_000_000 * (3 + steps), bytes_accessed=1024, transcendentals=0
        ),
        name="chip_sums",
    )(tables, owners(distances), core, adj, other_adj, *pieces)


def copy_rows_kernel(plans, n_sources, *refs):
    n_outs = len(plans)
    sources, outs, held = refs[:n_sources], refs[n_sources:-n_outs - 1], refs[-n_outs - 1 : -1]
    sems = refs[-1]
    loads, stores = [], []
    for out, buffer, plan in zip(outs, held, plans):
        place = 0
        for source, start, stop in plan:
            here, n = pl.ds(place, stop - start), len(loads)
            there = sources[source].at[pl.ds(start, stop - start)]
            loads.append(pltpu.make_async_copy(there, buffer.at[here], sems.at[0, n]))
            stores.append(pltpu.make_async_copy(buffer.at[here], out.at[here], sems.at[1, n]))
            place += stop - start
    for load in loads:
        load.start()
    for load, store in zip(loads, stores):
        load.wait()
        store.start()
    for store in stores:
        store.wait()


def copy_rows(sources, *plans):
    sizes = [(sum(stop - start for _, start, stop in plan), WIDTH) for plan in plans]
    dtype = sources[0].dtype
    any_spec = pl.BlockSpec(memory_space=pl.ANY)
    return pl.pallas_call(
        functools.partial(copy_rows_kernel, plans, len(sources)),
        out_shape=[jax.ShapeDtypeStruct(size, dtype) for size in sizes],
        in_specs=[any_spec] * len(sources),
        out_specs=[any_spec] * len(plans),
        scratch_shapes=[
            *[pltpu.VMEM(size, dtype) for size in sizes],
            pltpu.SemaphoreType.DMA((2, sum(len(plan) for plan in plans))),
        ],
        compiler_params=pltpu.CompilerParams(vmem_limit_bytes=60 * 1024 * 1024),
        name="copy_rows",
    )(*sources)


def together(*values):
    return lax.optimization_barrier(values)


def gather(own, shared, others):
    n = own.shape[0]
    half, first = n // 2, SIDE_FIRST * BS
    last, cut = n - first, SIDE_FIRST // 2 * BS
    up, down, side = permute(own, "y", 1), permute(own, "y", -1), permute(own, "xl", 1)
    shared = [permute(value, "core", 1) for value in shared]
    up, down, side, shared = together(up, down, side, shared)
    go_up, go_down, go_across = copy_rows(
        (up, down, side),
        ((0, 0, half), (2, 0, first)),
        ((1, half, n), (2, 0, first)),
        ((0, first, n), (1, first, n)),
    )
    via_up, via_down = permute(go_up, "y", 1), permute(go_down, "y", -1)
    across = permute(go_across, "xl", 1)
    others = others(up)
    via_up, via_down, across, others = together(via_up, via_down, across, others)
    ends = copy_rows(
        (via_up, via_down),
        ((0, half, half + cut),),
        ((1, half + cut, half + first),),
        ((1, first - half, half),),
    )
    end_up = permute(ends[0], "y", 1)
    end_down = permute(ends[1], "y", -1)
    end_across = permute(ends[2], "xl", 1)
    early = [own, up, down, side, via_up, via_down, across]
    late = [end_up, end_down, end_across]
    parts = [
        [(0, n, 0)],
        [(0, n, 3 * n)],
        [(0, n, n)],
        [(0, n, 4 * n)],
        [(0, half, 2 * n), (half, first, 7 * n)],
        [(0, half, 2 * n + half), (half, first, 5 * n)],
        [(0, last, 7 * n + first), (last, last, 5 * n + first)],
        [(0, cut, 6 * n)],
        [(0, first - cut, 6 * n + cut)],
        [(0, last, 6 * n + first)],
    ]
    pieces = early + late
    pieces += [permute(x, "core", 1) for x in pieces]
    layout = [(i, *part) for i, each in enumerate(parts) for part in each]
    layout += [(len(parts) + i, start, rows, place + 8 * n) for i, start, rows, place in layout]
    return layout, pieces, shared, others


def add_via_kernel(up_in, down_in, via_a, via_b, up, down, *refs):
    part = via_a.shape[1]
    held, (sems,) = refs[:-1], refs[-1:]
    targets = up.at[:, pl.ds(0, part)], down.at[:, pl.ds(part, via_b.shape[1])]
    sources = up_in.at[:, pl.ds(0, part)], down_in.at[:, pl.ds(part, via_b.shape[1])]
    loads = [
        pltpu.make_async_copy(source, buffer, sems.at[n])
        for n, (source, buffer) in enumerate(zip((*sources, via_a, via_b), held))
    ]
    for load in loads:
        load.start()
    stores = []
    for n in range(2):
        loads[n].wait()
        loads[n + 2].wait()
        total = held[n][...].astype(jnp.float32) + held[n + 2][...].astype(jnp.float32)
        held[n][...] = total.astype(jnp.bfloat16)
        stores.append(pltpu.make_async_copy(held[n], targets[n], sems.at[4 + n]))
        stores[n].start()
    for store in stores:
        store.wait()


def add_via(up, down, via_a, via_b):
    any_spec = pl.BlockSpec(memory_space=pl.ANY)
    return pl.pallas_call(
        add_via_kernel,
        out_shape=[jax.ShapeDtypeStruct(x.shape, x.dtype) for x in (up, down)],
        in_specs=[any_spec] * 4,
        out_specs=[any_spec] * 2,
        scratch_shapes=[
            *[pltpu.VMEM(x.shape, x.dtype) for x in (via_a, via_b, via_a, via_b)],
            pltpu.SemaphoreType.DMA((6,)),
        ],
        input_output_aliases={0: 0, 1: 1},
        compiler_params=pltpu.CompilerParams(vmem_limit_bytes=60 * 1024 * 1024),
        name="add_via",
    )(up, down, via_a, via_b)


def add(*terms):
    total = terms[0].astype(jnp.float32)
    for term in terms[1:]:
        total = total + term.astype(jnp.float32)
    return total.astype(jnp.bfloat16)


def reduce_to_owner(far, near, others):
    far_a, far_b, keep, give = far
    via_a = permute(far_a, "z", 1)
    via_b = permute(far_b, "z", -1)
    came = permute(give, "xh", 1)
    via_a, via_b, came, near = together(via_a, via_b, came, near)
    cut = came.shape[1] // 2
    high_a, high_b = add(keep[0, :cut], came[0, :cut]), add(keep[0, cut:], came[0, cut:])
    sums = high_a, high_b
    high_a, high_b = permute(high_a, "z", 1), permute(high_b, "z", -1)
    up, down, own, keep, give = near
    up, down = add_via(up, down, via_a, via_b)
    others = others((up, sums))
    came = permute(give, "xh", 1)
    up, down, came, high_a, high_b = together(
        permute(up, "z", 1), permute(down, "z", -1), came, high_a, high_b
    )
    low = add(own[1], up[1], down[1])
    low_side = permute(low, "xh", 1)
    (keep, came), _ = lax.optimization_barrier(((keep, came), low))
    rest = came.shape[1] - cut
    high_up = add(keep[0], came[0], jnp.pad(high_a, ((0, rest), (0, 0), (0, 0))))
    high_down = add(keep[1], came[1], jnp.pad(high_b, ((cut, 0), (0, 0), (0, 0))))
    (own, up, down, keep, came), _ = lax.optimization_barrier(
        ((own, up, down, keep, came), (high_up, high_down))
    )
    low_side, high_up, high_down, low, high = together(
        low_side,
        permute(high_up, "z", 1),
        permute(high_down, "z", -1),
        add(own[0], up[0], down[0]),
        add(keep[2], came[2]),
    )
    high = add(high, high_up, high_down)
    return jnp.concatenate([add(low, low_side), high]).reshape(-1, WIDTH), others


def derivative(preact, grad_rows):
    sigmoid_pre = jax.nn.sigmoid(preact)
    return (
        grad_rows.astype(jnp.float32) * sigmoid_pre * (1.0 + preact * (1.0 - sigmoid_pre))
    ).astype(jnp.bfloat16)


AXES = ("xl", "y", "xh", "z", "core")


def swap_all(rows, devices_all):
    return lax.all_to_all(
        rows.reshape(devices_all, -1, rows.shape[-1]), AXES, split_axis=0, concat_axis=0, tiled=True
    )


def on_device(features, weight, adj_rows, adj_cols, adj_blocks, counts, grad_out):
    local_rows, feat_width = features.shape
    devices_all = 128
    xl, y, xh, z, core = (lax.axis_index(name) for name in AXES)

    slots = jnp.arange(adj_rows.shape[-1], dtype=jnp.int32)
    rows = adj_rows.reshape(-1) - (slots % 16) * OWNER_BLOCKS
    cols = adj_cols.reshape(-1)
    source = cols // OWNER_BLOCKS
    away = ((source // 4) ^ xl) * 4 + (source % 4 - y) % 4
    cols = away * OWNER_BLOCKS + cols % OWNER_BLOCKS
    mine = jnp.stack([cols, rows, jnp.broadcast_to(counts.reshape(1), rows.shape)])

    def owners(distances):
        chips = [(xh ^ dx) * 4 + (z + dz) % 4 for dz in distances for dx in range(2)]
        return jnp.stack(chips).astype(jnp.int32)

    adj = adj_blocks.reshape(TURNS, PEERS, 2, BS, BS)
    other_adj = lax.dynamic_index_in_dim(adj, 1 - core, 2, keepdims=False)

    def tied(value, *others):
        return lax.optimization_barrier((value, others))[0]

    sub_rows = local_rows // devices_all

    def grads_first(after):
        grads = tied(grad_out, after).reshape(2, 4, 16, sub_rows, feat_width)
        grads = grads.transpose(0, 2, 1, 3, 4).reshape(32, 4, sub_rows, feat_width)
        return lax.all_to_all(grads, ("xl", "xh", "z", "core"), 0, 0, tiled=True)

    def grads_last(grads, after):
        grads = tied(grads, after).transpose(1, 0, 2, 3)
        grads = lax.all_to_all(grads, "y", 0, 0, tiled=True)
        grads = grads.reshape(4, 2, 16, sub_rows, feat_width).transpose(1, 0, 2, 3, 4)
        return grads.reshape(local_rows, feat_width)

    layout, pieces, (theirs, other_adj), grads = gather(features, (mine, other_adj), grads_first)
    tables = jnp.stack([mine, theirs.at[0].add(CB)])
    products = functools.partial(
        chip_sums, tables=tables, owners=owners, core=core.reshape(1), adj=adj, other_adj=other_adj
    )
    far = products((layout, pieces), (2,))

    near = products((layout, pieces), (1, 3, 0))
    agg, grad_row = reduce_to_owner(far, near, functools.partial(grads_last, grads))

    preact = jnp.dot(agg, weight, preferred_element_type=jnp.float32)
    out_row = jax.nn.silu(preact).astype(jnp.bfloat16)
    grad_pre = derivative(preact, grad_row)
    contract = (((0,), (0,)), ((), ()))
    weight_part = lax.dot_general(agg, grad_pre, contract, preferred_element_type=jnp.float32)
    coarse = lax.reduce_precision(weight_part, 8, 7)
    terms = [coarse.astype(jnp.bfloat16), (weight_part - coarse).astype(jnp.bfloat16)]
    lanes = [out_row[:, :BS], out_row[:, BS:], *terms]
    sent = jnp.concatenate([x.reshape(devices_all, -1, BS) for x in lanes], axis=1)
    came = lax.all_to_all(sent, AXES, split_axis=0, concat_axis=0, tiled=True)
    piece = local_rows // devices_all
    out_col = jnp.concatenate([came[:, :piece], came[:, piece : 2 * piece]], axis=2)
    out_col = out_col.reshape(local_rows, feat_width)
    came = came[:, 2 * piece :].astype(jnp.float32)
    each = came.shape[1] // 2
    summed = jnp.sum(came[:, :each] + came[:, each:], axis=0) * (local_rows * devices_all) ** (-0.5)
    summed = summed.reshape(-1, feat_width)
    spread = jnp.broadcast_to(summed[None], (devices_all, *summed.shape))
    weight_grad = lax.all_to_all(spread, AXES, split_axis=0, concat_axis=0, tiled=True)
    return (out_col, weight_grad.reshape(feat_width, feat_width))


def solution(mesh):
    fine = Mesh(mesh.devices.reshape(2, 4, 2, 4, 2), AXES)
    row, col = ("xl", "y"), ("xh", "z", "core")
    placed = (
        P((*col, *row), None),
        P(),
        P(row, col, None),
        P(row, col, None),
        P(row, col, None, None, None),
        P(row, col),
        P((*col, *row), None),
    )
    return jax.shard_map(
        on_device,
        mesh=fine,
        in_specs=placed,
        out_specs=(P((*col, *row), None), P()),
        check_vma=False,
    )
```

```python
import functools

import jax
import jax.numpy as jnp
from jax import lax
from jax.experimental import pallas as pl
from jax.experimental.pallas import tpu as pltpu
from jax.sharding import Mesh, PartitionSpec as P

BS = 128
WIDTH = 256
OWNER_BLOCKS = 16
LOW = 8
SIDE_FIRST = 10
TURNS = 8
PEERS = 8
CB = 128


def ring(size, step):
    return [(i, (i + step) % size) for i in range(size)]


def permute(value, axis, step):
    return lax.ppermute(value, axis, ring(lax.axis_size(axis), step))


def slab_copies(layout, pieces, slab, sems):
    return [
        pltpu.make_async_copy(
            pieces[piece].at[pl.ds(start, rows)], slab.at[pl.ds(place, rows)], sems.at[n]
        )
        for n, (piece, start, rows, place) in enumerate(layout)
    ]


def chip_kernel(
    layout, n_pieces, stores, tables, owners, core, adj_ref, other_adj_ref, *refs
):
    pieces, outs, (slab, sums, sems) = refs[:n_pieces], refs[n_pieces:-3], refs[-3:]
    step = pl.program_id(0)

    @pl.when(step == 0)
    def _():
        for copy in slab_copies(layout, pieces, slab, sems):
            copy.start()
        for copy in slab_copies(layout, pieces, slab, sems)[: len(layout) // 2]:
            copy.wait()

    sums[...] = jnp.zeros_like(sums)

    def product(cell, slot, block):
        start = pl.multiple_of(tables[cell, 0, slot] * BS, BS)
        found = jnp.dot(block, slab[pl.ds(start, BS), :], preferred_element_type=jnp.float32)
        return jnp.where(slot < tables[cell, 2, 0], found, 0.0).astype(jnp.bfloat16)

    slots = [turn * 16 + owners[step] * 2 + core[0] for turn in range(TURNS)]
    for turn, slot in enumerate(slots):
        sums[tables[0, 1, slot]] = product(0, slot, adj_ref[turn, 0, 0])

    @pl.when(step == 0)
    def _():
        for copy in slab_copies(layout, pieces, slab, sems)[len(layout) // 2 :]:
            copy.wait()

    for turn, slot in enumerate(slots):
        row = tables[1, 1, slot]
        term = product(1, slot, other_adj_ref[turn, 0, 0]).astype(jnp.float32)
        sums[row] = (sums[row].astype(jnp.float32) + term).astype(jnp.bfloat16)

    for out, (first, last, start, stop, every) in zip(outs, stores):

        @pl.when((step >= first) & (step < last) & ((step - first) % every == 0))
        def _():
            out[0] = sums[start:stop]


def chip_sums(gathered, distances, tables, owners, core, adj, other_adj):
    layout, pieces = gathered
    steps = 2 * len(distances)
    high = OWNER_BLOCKS - LOW
    shapes, specs, stores = [], [], []

    def output(count, blocks, place, store):
        shapes.append(jax.ShapeDtypeStruct((count, blocks, BS, WIDTH), jnp.bfloat16))
        specs.append(pl.BlockSpec((1, blocks, BS, WIDTH), lambda g, *_: (place(g), 0, 0, 0)))
        stores.append(store)

    for n, distance in enumerate(distances):
        cuts = (0, LOW // 2, LOW) if distance == 2 else (0, LOW)
        for start, stop in zip(cuts, cuts[1:]):
            output(
                2,
                stop - start,
                lambda g, first=2 * n: jnp.clip(g - first, 0, 1),
                (2 * n, 2 * n + 2, start, stop, 1),
            )
    for side in range(2):
        output(len(distances), high, lambda g: g // 2, (side, steps, LOW, OWNER_BLOCKS, 2))
    return pl.pallas_call(
        functools.partial(chip_kernel, layout, len(pieces), stores),
        out_shape=shapes,
        grid_spec=pltpu.PrefetchScalarGridSpec(
            num_scalar_prefetch=3,
            grid=(steps,),
            in_specs=[
                pl.BlockSpec((TURNS, 1, 1, BS, BS), lambda g, tb, ow, co: (0, ow[g], co[0], 0, 0)),
                pl.BlockSpec((TURNS, 1, 1, BS, BS), lambda g, tb, ow, co: (0, ow[g], co[0], 0, 0)),
                *[pl.BlockSpec(memory_space=pl.ANY)] * len(pieces),
            ],
            out_specs=specs,
            scratch_shapes=[
                pltpu.VMEM((2 * CB * BS, WIDTH), jnp.bfloat16),
                pltpu.VMEM((OWNER_BLOCKS, BS, WIDTH), jnp.bfloat16),
                pltpu.SemaphoreType.DMA((len(layout),)),
            ],
        ),
        compiler_params=pltpu.CompilerParams(
            dimension_semantics=("arbitrary",), vmem_limit_bytes=60 * 1024 * 1024
        ),
        cost_estimate=pl.CostEstimate(
            flops=2_000_000_000 * (3 + steps), bytes_accessed=1024, transcendentals=0
        ),
        name="chip_sums",
    )(tables, owners(distances), core, adj, other_adj, *pieces)


def copy_rows_kernel(plans, n_sources, *refs):
    n_outs = len(plans)
    sources, outs, held = refs[:n_sources], refs[n_sources:-n_outs - 1], refs[-n_outs - 1 : -1]
    sems = refs[-1]
    loads, stores = [], []
    for out, buffer, plan in zip(outs, held, plans):
        place = 0
        for source, start, stop in plan:
            here, n = pl.ds(place, stop - start), len(loads)
            there = sources[source].at[pl.ds(start, stop - start)]
            loads.append(pltpu.make_async_copy(there, buffer.at[here], sems.at[0, n]))
            stores.append(pltpu.make_async_copy(buffer.at[here], out.at[here], sems.at[1, n]))
            place += stop - start
    for load in loads:
        load.start()
    for load, store in zip(loads, stores):
        load.wait()
        store.start()
    for store in stores:
        store.wait()


def copy_rows(sources, *plans):
    sizes = [(sum(stop - start for _, start, stop in plan), WIDTH) for plan in plans]
    dtype = sources[0].dtype
    any_spec = pl.BlockSpec(memory_space=pl.ANY)
    return pl.pallas_call(
        functools.partial(copy_rows_kernel, plans, len(sources)),
        out_shape=[jax.ShapeDtypeStruct(size, dtype) for size in sizes],
        in_specs=[any_spec] * len(sources),
        out_specs=[any_spec] * len(plans),
        scratch_shapes=[
            *[pltpu.VMEM(size, dtype) for size in sizes],
            pltpu.SemaphoreType.DMA((2, sum(len(plan) for plan in plans))),
        ],
        compiler_params=pltpu.CompilerParams(vmem_limit_bytes=60 * 1024 * 1024),
        name="copy_rows",
    )(*sources)


def together(*values):
    return lax.optimization_barrier(values)


def gather(own, shared, others):
    n = own.shape[0]
    half, first = n // 2, SIDE_FIRST * BS
    last, cut = n - first, SIDE_FIRST // 2 * BS
    up, down, side = permute(own, "y", 1), permute(own, "y", -1), permute(own, "xl", 1)
    shared = [permute(value, "core", 1) for value in shared]
    up, down, side, shared = together(up, down, side, shared)
    go_up, go_down, go_across = copy_rows(
        (up, down, side),
        ((0, 0, half), (2, 0, first)),
        ((1, half, n), (2, 0, first)),
        ((0, first, n), (1, first, n)),
    )
    via_up, via_down = permute(go_up, "y", 1), permute(go_down, "y", -1)
    across = permute(go_across, "xl", 1)
    others = others(up)
    via_up, via_down, across, others = together(via_up, via_down, across, others)
    ends = copy_rows(
        (via_up, via_down),
        ((0, half, half + cut),),
        ((1, half + cut, half + first),),
        ((1, first - half, half),),
    )
    end_up = permute(ends[0], "y", 1)
    end_down = permute(ends[1], "y", -1)
    end_across = permute(ends[2], "xl", 1)
    early = [own, up, down, side, via_up, via_down, across]
    late = [end_up, end_down, end_across]
    parts = [
        [(0, n, 0)],
        [(0, n, 3 * n)],
        [(0, n, n)],
        [(0, n, 4 * n)],
        [(0, half, 2 * n), (half, first, 7 * n)],
        [(0, half, 2 * n + half), (half, first, 5 * n)],
        [(0, last, 7 * n + first), (last, last, 5 * n + first)],
        [(0, cut, 6 * n)],
        [(0, first - cut, 6 * n + cut)],
        [(0, last, 6 * n + first)],
    ]
    pieces = early + late
    pieces += [permute(x, "core", 1) for x in pieces]
    layout = [(i, *part) for i, each in enumerate(parts) for part in each]
    layout += [(len(parts) + i, start, rows, place + 8 * n) for i, start, rows, place in layout]
    return layout, pieces, shared, others


def add_via_kernel(up_in, down_in, via_a, via_b, up, down, *refs):
    part = via_a.shape[1]
    held, (sems,) = refs[:-1], refs[-1:]
    targets = up.at[:, pl.ds(0, part)], down.at[:, pl.ds(part, via_b.shape[1])]
    sources = up_in.at[:, pl.ds(0, part)], down_in.at[:, pl.ds(part, via_b.shape[1])]
    loads = [
        pltpu.make_async_copy(source, buffer, sems.at[n])
        for n, (source, buffer) in enumerate(zip((*sources, via_a, via_b), held))
    ]
    for load in loads:
        load.start()
    stores = []
    for n in range(2):
        loads[n].wait()
        loads[n + 2].wait()
        total = held[n][...].astype(jnp.float32) + held[n + 2][...].astype(jnp.float32)
        held[n][...] = total.astype(jnp.bfloat16)
        stores.append(pltpu.make_async_copy(held[n], targets[n], sems.at[4 + n]))
        stores[n].start()
    for store in stores:
        store.wait()


def add_via(up, down, via_a, via_b):
    any_spec = pl.BlockSpec(memory_space=pl.ANY)
    return pl.pallas_call(
        add_via_kernel,
        out_shape=[jax.ShapeDtypeStruct(x.shape, x.dtype) for x in (up, down)],
        in_specs=[any_spec] * 4,
        out_specs=[any_spec] * 2,
        scratch_shapes=[
            *[pltpu.VMEM(x.shape, x.dtype) for x in (via_a, via_b, via_a, via_b)],
            pltpu.SemaphoreType.DMA((6,)),
        ],
        input_output_aliases={0: 0, 1: 1},
        compiler_params=pltpu.CompilerParams(vmem_limit_bytes=60 * 1024 * 1024),
        name="add_via",
    )(up, down, via_a, via_b)


def add(*terms):
    total = terms[0].astype(jnp.float32)
    for term in terms[1:]:
        total = total + term.astype(jnp.float32)
    return total.astype(jnp.bfloat16)


def reduce_to_owner(far, near, others):
    far_a, far_b, keep, give = far
    via_a = permute(far_a, "z", 1)
    via_b = permute(far_b, "z", -1)
    came = permute(give, "xh", 1)
    via_a, via_b, came, near = together(via_a, via_b, came, near)
    cut = came.shape[1] // 2
    high_a, high_b = add(keep[0, :cut], came[0, :cut]), add(keep[0, cut:], came[0, cut:])
    sums = high_a, high_b
    high_a, high_b = permute(high_a, "z", 1), permute(high_b, "z", -1)
    up, down, own, keep, give = near
    up, down = add_via(up, down, via_a, via_b)
    others = others((up, sums))
    came = permute(give, "xh", 1)
    up, down, came, high_a, high_b = together(
        permute(up, "z", 1), permute(down, "z", -1), came, high_a, high_b
    )
    low = add(own[1], up[1], down[1])
    low_side = permute(low, "xh", 1)
    (keep, came), _ = lax.optimization_barrier(((keep, came), low))
    rest = came.shape[1] - cut
    high_up = add(keep[0], came[0], jnp.pad(high_a, ((0, rest), (0, 0), (0, 0))))
    high_down = add(keep[1], came[1], jnp.pad(high_b, ((cut, 0), (0, 0), (0, 0))))
    (own, up, down, keep, came), _ = lax.optimization_barrier(
        ((own, up, down, keep, came), (high_up, high_down))
    )
    low_side, high_up, high_down, low, high = together(
        low_side,
        permute(high_up, "z", 1),
        permute(high_down, "z", -1),
        add(own[0], up[0], down[0]),
        add(keep[2], came[2]),
    )
    high = add(high, high_up, high_down)
    return jnp.concatenate([add(low, low_side), high]).reshape(-1, WIDTH), others


def derivative(preact, grad_rows):
    sigmoid_pre = jax.nn.sigmoid(preact)
    return (
        grad_rows.astype(jnp.float32) * sigmoid_pre * (1.0 + preact * (1.0 - sigmoid_pre))
    ).astype(jnp.bfloat16)


AXES = ("xl", "y", "xh", "z", "core")


def swap_all(rows, devices_all):
    return lax.all_to_all(
        rows.reshape(devices_all, -1, rows.shape[-1]), AXES, split_axis=0, concat_axis=0, tiled=True
    )


def on_device(features, weight, adj_rows, adj_cols, adj_blocks, counts, grad_out):
    local_rows, feat_width = features.shape
    devices_all = 128
    xl, y, xh, z, core = (lax.axis_index(name) for name in AXES)

    slots = jnp.arange(adj_rows.shape[-1], dtype=jnp.int32)
    rows = adj_rows.reshape(-1) - (slots % 16) * OWNER_BLOCKS
    cols = adj_cols.reshape(-1)
    source = cols // OWNER_BLOCKS
    away = ((source // 4) ^ xl) * 4 + (source % 4 - y) % 4
    cols = away * OWNER_BLOCKS + cols % OWNER_BLOCKS
    mine = jnp.stack([cols, rows, jnp.broadcast_to(counts.reshape(1), rows.shape)])

    def owners(distances):
        chips = [(xh ^ dx) * 4 + (z + dz) % 4 for dz in distances for dx in range(2)]
        return jnp.stack(chips).astype(jnp.int32)

    adj = adj_blocks.reshape(TURNS, PEERS, 2, BS, BS)

    def tied(value, *others):
        return lax.optimization_barrier((value, others))[0]

    sub_rows = local_rows // devices_all

    def grads_first(after):
        grads = tied(grad_out, after).reshape(2, 4, 16, sub_rows, feat_width)
        grads = grads.transpose(0, 2, 1, 3, 4).reshape(32, 4, sub_rows, feat_width)
        return lax.all_to_all(grads, ("xl", "xh", "z", "core"), 0, 0, tiled=True)

    def grads_last(grads, after):
        grads = tied(grads, after).transpose(1, 0, 2, 3)
        grads = lax.all_to_all(grads, "y", 0, 0, tiled=True)
        grads = grads.reshape(4, 2, 16, sub_rows, feat_width).transpose(1, 0, 2, 3, 4)
        return grads.reshape(local_rows, feat_width)

    layout, pieces, (theirs, other_adj), grads = gather(features, (mine, adj), grads_first)
    tables = jnp.stack([mine, theirs.at[0].add(CB)])
    products = functools.partial(
        chip_sums, tables=tables, owners=owners, core=core.reshape(1), adj=adj, other_adj=other_adj
    )
    far = products((layout, pieces), (2,))

    near = products((layout, pieces), (1, 3, 0))
    agg, grad_row = reduce_to_owner(far, near, functools.partial(grads_last, grads))

    preact = jnp.dot(agg, weight, preferred_element_type=jnp.float32)
    out_row = jax.nn.silu(preact).astype(jnp.bfloat16)
    grad_pre = derivative(preact, grad_row)
    contract = (((0,), (0,)), ((), ()))
    weight_part = lax.dot_general(agg, grad_pre, contract, preferred_element_type=jnp.float32)
    coarse = lax.reduce_precision(weight_part, 8, 7)
    terms = [coarse.astype(jnp.bfloat16), (weight_part - coarse).astype(jnp.bfloat16)]
    lanes = [out_row[:, :BS], out_row[:, BS:], *terms]
    sent = jnp.concatenate([x.reshape(devices_all, -1, BS) for x in lanes], axis=1)
    came = lax.all_to_all(sent, AXES, split_axis=0, concat_axis=0, tiled=True)
    piece = local_rows // devices_all
    out_col = jnp.concatenate([came[:, :piece], came[:, piece : 2 * piece]], axis=2)
    out_col = out_col.reshape(local_rows, feat_width)
    came = came[:, 2 * piece :].astype(jnp.float32)
    each = came.shape[1] // 2
    summed = jnp.sum(came[:, :each] + came[:, each:], axis=0) * (local_rows * devices_all) ** (-0.5)
    summed = summed.reshape(-1, feat_width)
    spread = jnp.broadcast_to(summed[None], (devices_all, *summed.shape))
    weight_grad = lax.all_to_all(spread, AXES, split_axis=0, concat_axis=0, tiled=True)
    return (out_col, weight_grad.reshape(feat_width, feat_width))


def solution(mesh):
    fine = Mesh(mesh.devices.reshape(2, 4, 2, 4, 2), AXES)
    row, col = ("xl", "y"), ("xh", "z", "core")
    placed = (
        P((*col, *row), None),
        P(),
        P(row, col, None),
        P(row, col, None),
        P(row, col, None, None, None),
        P(row, col),
        P((*col, *row), None),
    )
    return jax.shard_map(
        on_device,
        mesh=fine,
        in_specs=placed,
        out_specs=(P((*col, *row), None), P()),
        check_vma=False,
    )
```

```python
import functools

import jax
import jax.numpy as jnp
from jax import lax
from jax.experimental import pallas as pl
from jax.experimental.pallas import tpu as pltpu
from jax.sharding import Mesh, PartitionSpec as P

BS = 128
WIDTH = 256
OWNER_BLOCKS = 16
LOW = 8
SIDE_FIRST = 10
TURNS = 8
PEERS = 8
CB = 128


def ring(size, step):
    return [(i, (i + step) % size) for i in range(size)]


def permute(value, axis, step):
    return lax.ppermute(value, axis, ring(lax.axis_size(axis), step))


def slab_copies(layout, pieces, slab, sems):
    return [
        pltpu.make_async_copy(
            pieces[piece].at[pl.ds(start, rows)], slab.at[pl.ds(place, rows)], sems.at[n]
        )
        for n, (piece, start, rows, place) in enumerate(layout)
    ]


def chip_kernel(
    layout, n_pieces, stores, tables, owners, core, adj_ref, other_adj_ref, *refs
):
    pieces, outs, (slab, sums, sems) = refs[:n_pieces], refs[n_pieces:-3], refs[-3:]
    step = pl.program_id(0)

    @pl.when(step == 0)
    def _():
        for copy in slab_copies(layout, pieces, slab, sems):
            copy.start()
        for copy in slab_copies(layout, pieces, slab, sems)[: len(layout) // 2]:
            copy.wait()

    sums[...] = jnp.zeros_like(sums)

    def product(cell, slot, block):
        start = pl.multiple_of(tables[cell, 0, slot] * BS, BS)
        found = jnp.dot(block, slab[pl.ds(start, BS), :], preferred_element_type=jnp.float32)
        return jnp.where(slot < tables[cell, 2, 0], found, 0.0).astype(jnp.bfloat16)

    slots = [turn * 16 + owners[step] * 2 + core[0] for turn in range(TURNS)]
    for turn, slot in enumerate(slots):
        sums[tables[0, 1, slot]] = product(0, slot, adj_ref[turn, 0, 0])

    @pl.when(step == 0)
    def _():
        for copy in slab_copies(layout, pieces, slab, sems)[len(layout) // 2 :]:
            copy.wait()

    for turn, slot in enumerate(slots):
        row = tables[1, 1, slot]
        term = product(1, slot, other_adj_ref[turn, 0, 0]).astype(jnp.float32)
        sums[row] = (sums[row].astype(jnp.float32) + term).astype(jnp.bfloat16)

    for out, (first, last, start, stop, every) in zip(outs, stores):

        @pl.when((step >= first) & (step < last) & ((step - first) % every == 0))
        def _():
            out[0] = sums[start:stop]


def chip_sums(gathered, distances, tables, owners, core, adj, other_adj):
    layout, pieces = gathered
    steps = 2 * len(distances)
    high = OWNER_BLOCKS - LOW
    shapes, specs, stores = [], [], []

    def output(count, blocks, place, store):
        shapes.append(jax.ShapeDtypeStruct((count, blocks, BS, WIDTH), jnp.bfloat16))
        specs.append(pl.BlockSpec((1, blocks, BS, WIDTH), lambda g, *_: (place(g), 0, 0, 0)))
        stores.append(store)

    for n, distance in enumerate(distances):
        cuts = (0, LOW // 2, LOW) if distance == 2 else (0, LOW)
        for start, stop in zip(cuts, cuts[1:]):
            output(
                2,
                stop - start,
                lambda g, first=2 * n: jnp.clip(g - first, 0, 1),
                (2 * n, 2 * n + 2, start, stop, 1),
            )
    for side in range(2):
        output(len(distances), high, lambda g: g // 2, (side, steps, LOW, OWNER_BLOCKS, 2))
    return pl.pallas_call(
        functools.partial(chip_kernel, layout, len(pieces), stores),
        out_shape=shapes,
        grid_spec=pltpu.PrefetchScalarGridSpec(
            num_scalar_prefetch=3,
            grid=(steps,),
            in_specs=[
                pl.BlockSpec((TURNS, 1, 1, BS, BS), lambda g, tb, ow, co: (0, ow[g], co[0], 0, 0)),
                pl.BlockSpec((TURNS, 1, 1, BS, BS), lambda g, tb, ow, co: (0, ow[g], co[0], 0, 0)),
                *[pl.BlockSpec(memory_space=pl.ANY)] * len(pieces),
            ],
            out_specs=specs,
            scratch_shapes=[
                pltpu.VMEM((2 * CB * BS, WIDTH), jnp.bfloat16),
                pltpu.VMEM((OWNER_BLOCKS, BS, WIDTH), jnp.bfloat16),
                pltpu.SemaphoreType.DMA((len(layout),)),
            ],
        ),
        compiler_params=pltpu.CompilerParams(
            dimension_semantics=("arbitrary",), vmem_limit_bytes=60 * 1024 * 1024
        ),
        cost_estimate=pl.CostEstimate(
            flops=2_000_000_000 * (3 + steps), bytes_accessed=1024, transcendentals=0
        ),
        name="chip_sums",
    )(tables, owners(distances), core, adj, other_adj, *pieces)


def copy_rows_kernel(plans, n_sources, *refs):
    n_outs = len(plans)
    sources, outs, held = refs[:n_sources], refs[n_sources:-n_outs - 1], refs[-n_outs - 1 : -1]
    sems = refs[-1]
    loads, stores = [], []
    for out, buffer, plan in zip(outs, held, plans):
        place = 0
        for source, start, stop in plan:
            here, n = pl.ds(place, stop - start), len(loads)
            there = sources[source].at[pl.ds(start, stop - start)]
            loads.append(pltpu.make_async_copy(there, buffer.at[here], sems.at[0, n]))
            stores.append(pltpu.make_async_copy(buffer.at[here], out.at[here], sems.at[1, n]))
            place += stop - start
    for load in loads:
        load.start()
    for load, store in zip(loads, stores):
        load.wait()
        store.start()
    for store in stores:
        store.wait()


def copy_rows(sources, *plans):
    sizes = [(sum(stop - start for _, start, stop in plan), WIDTH) for plan in plans]
    dtype = sources[0].dtype
    any_spec = pl.BlockSpec(memory_space=pl.ANY)
    return pl.pallas_call(
        functools.partial(copy_rows_kernel, plans, len(sources)),
        out_shape=[jax.ShapeDtypeStruct(size, dtype) for size in sizes],
        in_specs=[any_spec] * len(sources),
        out_specs=[any_spec] * len(plans),
        scratch_shapes=[
            *[pltpu.VMEM(size, dtype) for size in sizes],
            pltpu.SemaphoreType.DMA((2, sum(len(plan) for plan in plans))),
        ],
        compiler_params=pltpu.CompilerParams(vmem_limit_bytes=60 * 1024 * 1024),
        name="copy_rows",
    )(*sources)


def together(*values):
    return lax.optimization_barrier(values)


def gather(own, shared, others):
    n = own.shape[0]
    half, first = n // 2, SIDE_FIRST * BS
    last, cut = n - first, SIDE_FIRST // 2 * BS
    up, down, side = permute(own, "y", 1), permute(own, "y", -1), permute(own, "xl", 1)
    shared = [permute(value, "core", 1) for value in shared]
    up, down, side, shared = together(up, down, side, shared)
    go_up, go_down, go_across = copy_rows(
        (up, down, side),
        ((0, 0, half), (2, 0, first)),
        ((1, half, n), (2, 0, first)),
        ((0, first, n), (1, first, n)),
    )
    via_up, via_down = permute(go_up, "y", 1), permute(go_down, "y", -1)
    across = permute(go_across, "xl", 1)
    others = others(up)
    via_up, via_down, across, others = together(via_up, via_down, across, others)
    ends = copy_rows(
        (via_up, via_down),
        ((0, half, half + cut),),
        ((1, half + cut, half + first),),
        ((1, first - half, half),),
    )
    end_up = permute(ends[0], "y", 1)
    end_down = permute(ends[1], "y", -1)
    end_across = permute(ends[2], "xl", 1)
    early = [own, up, down, side, via_up, via_down, across]
    late = [end_up, end_down, end_across]
    parts = [
        [(0, n, 0)],
        [(0, n, 3 * n)],
        [(0, n, n)],
        [(0, n, 4 * n)],
        [(0, half, 2 * n), (half, first, 7 * n)],
        [(0, half, 2 * n + half), (half, first, 5 * n)],
        [(0, last, 7 * n + first), (last, last, 5 * n + first)],
        [(0, cut, 6 * n)],
        [(0, first - cut, 6 * n + cut)],
        [(0, last, 6 * n + first)],
    ]
    pieces = early + late
    pieces += [permute(x, "core", 1) for x in pieces]
    layout = [(i, *part) for i, each in enumerate(parts) for part in each]
    layout += [(len(parts) + i, start, rows, place + 8 * n) for i, start, rows, place in layout]
    return layout, pieces, shared, others


def add_via_kernel(up_in, down_in, via_a, via_b, up, down, *refs):
    part = via_a.shape[1]
    held, (sems,) = refs[:-1], refs[-1:]
    targets = up.at[:, pl.ds(0, part)], down.at[:, pl.ds(part, via_b.shape[1])]
    sources = up_in.at[:, pl.ds(0, part)], down_in.at[:, pl.ds(part, via_b.shape[1])]
    loads = [
        pltpu.make_async_copy(source, buffer, sems.at[n])
        for n, (source, buffer) in enumerate(zip((*sources, via_a, via_b), held))
    ]
    for load in loads:
        load.start()
    stores = []
    for n in range(2):
        loads[n].wait()
        loads[n + 2].wait()
        total = held[n][...].astype(jnp.float32) + held[n + 2][...].astype(jnp.float32)
        held[n][...] = total.astype(jnp.bfloat16)
        stores.append(pltpu.make_async_copy(held[n], targets[n], sems.at[4 + n]))
        stores[n].start()
    for store in stores:
        store.wait()


def add_via(up, down, via_a, via_b):
    any_spec = pl.BlockSpec(memory_space=pl.ANY)
    return pl.pallas_call(
        add_via_kernel,
        out_shape=[jax.ShapeDtypeStruct(x.shape, x.dtype) for x in (up, down)],
        in_specs=[any_spec] * 4,
        out_specs=[any_spec] * 2,
        scratch_shapes=[
            *[pltpu.VMEM(x.shape, x.dtype) for x in (via_a, via_b, via_a, via_b)],
            pltpu.SemaphoreType.DMA((6,)),
        ],
        input_output_aliases={0: 0, 1: 1},
        compiler_params=pltpu.CompilerParams(vmem_limit_bytes=60 * 1024 * 1024),
        name="add_via",
    )(up, down, via_a, via_b)


def add(*terms):
    total = terms[0].astype(jnp.float32)
    for term in terms[1:]:
        total = total + term.astype(jnp.float32)
    return total.astype(jnp.bfloat16)


def reduce_to_owner(far, near, others):
    far_a, far_b, keep, give = far
    via_a = permute(far_a, "z", 1)
    via_b = permute(far_b, "z", -1)
    came = permute(give, "xh", 1)
    via_a, via_b, came, near = together(via_a, via_b, came, near)
    cut = came.shape[1] // 2
    high_a, high_b = add(keep[0, :cut], came[0, :cut]), add(keep[0, cut:], came[0, cut:])
    sums = high_a, high_b
    high_a, high_b = permute(high_a, "z", 1), permute(high_b, "z", -1)
    up, down, own, keep, give = near
    up, down = add_via(up, down, via_a, via_b)
    others = others((up, sums))
    came = permute(give, "xh", 1)
    up, down, came, high_a, high_b = together(
        permute(up, "z", 1), permute(down, "z", -1), came, high_a, high_b
    )
    low = add(own[1], up[1], down[1])
    low_side = permute(low, "xh", 1)
    (keep, came), _ = lax.optimization_barrier(((keep, came), low))
    rest = came.shape[1] - cut
    high_up = add(keep[0], came[0], jnp.pad(high_a, ((0, rest), (0, 0), (0, 0))))
    high_down = add(keep[1], came[1], jnp.pad(high_b, ((cut, 0), (0, 0), (0, 0))))
    (own, up, down, keep, came), _ = lax.optimization_barrier(
        ((own, up, down, keep, came), (high_up, high_down))
    )
    low_side, high_up, high_down, low, high = together(
        low_side,
        permute(high_up, "z", 1),
        permute(high_down, "z", -1),
        add(own[0], up[0], down[0]),
        add(keep[2], came[2]),
    )
    high = add(high, high_up, high_down)
    return jnp.concatenate([add(low, low_side), high]).reshape(-1, WIDTH), others


def derivative(preact, grad_rows):
    sigmoid_pre = jax.nn.sigmoid(preact)
    return (
        grad_rows.astype(jnp.float32) * sigmoid_pre * (1.0 + preact * (1.0 - sigmoid_pre))
    ).astype(jnp.bfloat16)


AXES = ("xl", "y", "xh", "z", "core")


def swap_all(rows, devices_all):
    return lax.all_to_all(
        rows.reshape(devices_all, -1, rows.shape[-1]), AXES, split_axis=0, concat_axis=0, tiled=True
    )


def on_device(features, weight, adj_rows, adj_cols, adj_blocks, counts, grad_out):
    local_rows, feat_width = features.shape
    devices_all = 128
    xl, y, xh, z, core = (lax.axis_index(name) for name in AXES)

    slots = jnp.arange(adj_rows.shape[-1], dtype=jnp.int32)
    rows = adj_rows.reshape(-1) - (slots % 16) * OWNER_BLOCKS
    cols = adj_cols.reshape(-1)
    source = cols // OWNER_BLOCKS
    away = ((source // 4) ^ xl) * 4 + (source % 4 - y) % 4
    cols = away * OWNER_BLOCKS + cols % OWNER_BLOCKS
    mine = jnp.stack([cols, rows, jnp.broadcast_to(counts.reshape(1), rows.shape)])

    def owners(distances):
        chips = [(xh ^ dx) * 4 + (z + dz) % 4 for dz in distances for dx in range(2)]
        return jnp.stack(chips).astype(jnp.int32)

    adj = adj_blocks.reshape(TURNS, PEERS, 2, BS, BS)

    def tied(value, *others):
        return lax.optimization_barrier((value, others))[0]

    sub_rows = local_rows // devices_all

    def grads_first(after):
        grads = tied(grad_out, after).reshape(2, 4, 16, sub_rows, feat_width)
        grads = grads.transpose(0, 2, 1, 3, 4).reshape(32, 4, sub_rows, feat_width)
        return lax.all_to_all(grads, ("xl", "xh", "z", "core"), 0, 0, tiled=True)

    def grads_last(grads, after):
        grads = tied(grads.transpose(1, 0, 2, 3), after)
        grads = lax.all_to_all(grads, "y", 0, 0, tiled=True)
        grads = grads.reshape(4, 2, 16, sub_rows, feat_width).transpose(1, 0, 2, 3, 4)
        return grads.reshape(local_rows, feat_width)

    layout, pieces, (theirs, other_adj), grads = gather(features, (mine, adj), grads_first)
    tables = jnp.stack([mine, theirs.at[0].add(CB)])
    products = functools.partial(
        chip_sums, tables=tables, owners=owners, core=core.reshape(1), adj=adj, other_adj=other_adj
    )
    far = products((layout, pieces), (2,))

    near = products((layout, pieces), (1, 3, 0))
    agg, grad_row = reduce_to_owner(far, near, functools.partial(grads_last, grads))

    preact = jnp.dot(agg, weight, preferred_element_type=jnp.float32)
    out_row = jax.nn.silu(preact).astype(jnp.bfloat16)
    grad_pre = derivative(preact, grad_row)
    contract = (((0,), (0,)), ((), ()))
    weight_part = lax.dot_general(agg, grad_pre, contract, preferred_element_type=jnp.float32)
    coarse = lax.reduce_precision(weight_part, 8, 7)
    terms = [coarse.astype(jnp.bfloat16), (weight_part - coarse).astype(jnp.bfloat16)]
    lanes = [out_row[:, :BS], out_row[:, BS:], *terms]
    sent = jnp.concatenate([x.reshape(devices_all, -1, BS) for x in lanes], axis=1)
    came = lax.all_to_all(sent, AXES, split_axis=0, concat_axis=0, tiled=True)
    piece = local_rows // devices_all
    out_col = jnp.concatenate([came[:, :piece], came[:, piece : 2 * piece]], axis=2)
    out_col = out_col.reshape(local_rows, feat_width)
    came = came[:, 2 * piece :].astype(jnp.float32)
    each = came.shape[1] // 2
    summed = jnp.sum(came[:, :each] + came[:, each:], axis=0) * (local_rows * devices_all) ** (-0.5)
    summed = summed.reshape(-1, feat_width)
    spread = jnp.broadcast_to(summed[None], (devices_all, *summed.shape))
    weight_grad = lax.all_to_all(spread, AXES, split_axis=0, concat_axis=0, tiled=True)
    return (out_col, weight_grad.reshape(feat_width, feat_width))


def solution(mesh):
    fine = Mesh(mesh.devices.reshape(2, 4, 2, 4, 2), AXES)
    row, col = ("xl", "y"), ("xh", "z", "core")
    placed = (
        P((*col, *row), None),
        P(),
        P(row, col, None),
        P(row, col, None),
        P(row, col, None, None, None),
        P(row, col),
        P((*col, *row), None),
    )
    return jax.shard_map(
        on_device,
        mesh=fine,
        in_specs=placed,
        out_specs=(P((*col, *row), None), P()),
        check_vma=False,
    )
```
